32 devices in a mesh: dp: 8 (over y, x, core), mp: 4 (over z).
Axes of the slice: x: 2, y: 2, z: 4, core: 2. Of those that a mesh axis runs over, the one named last changes fastest.
Arguments:
- hidden: bfloat16 [32, 512, 1024], P(('dp', 'mp')), may hold values from -90 to 90
- positions: int32 [32, 80], P(('dp', 'mp')), may hold values from 0 to 511, as said below
- targets: int32 [32, 80], P(('dp', 'mp')), may hold values from 0 to 32767
- counts: int32 [32], P(('dp', 'mp')), may hold values from 1 to 80, 1920 in all
- dense_weight: bfloat16 [1024, 1024], replicated, may hold values from -1 to 1
- dense_bias: float32 [1024], replicated, may hold values from -3 to 3
- norm_gain: float32 [1024], replicated, may hold values from 0.4 to 1.6
- norm_shift: float32 [1024], replicated, may hold values from -3 to 3
- embedding: bfloat16 [32768, 1024], P('mp', 'dp'), may hold values from -2 to 2
- vocab_bias: float32 [32768], P('mp'), may hold values from -5 to 5
Outputs:
- loss: float32 [], replicated
- embedding_grad: float32 [32768, 1024], P('mp', 'dp')
The draws below stay inside these ranges and needn't reach their ends.
Inputs may be any that keep to these rules, and one draw needn't show every extreme that they name: The 80 positions of a sequence are distinct; only the first counts[s] of them are masked. `counts`: some sequence has exactly 80.
All inputs are finite; a program needn't handle non-finite values. No bound on the sum of `counts` on one device may be relied on, other than what follows from the above.
Results may differ from the reference program's by a relative error of at most 0.00041.
Values may be sent and summed in bfloat16 or wider, within the bound.
No kernel may reach another device: no remote copies, remote signals or barrier semaphores. Data moves between devices by JAX's collectives and lax.ppermute only.
A program may use at most 128 MiB of HBM per device.

```python
import math
import jax
import jax.numpy as jnp
import numpy as np
from jax import lax

D = 1024
VOCAB = 32768
SEQ_LEN = 512
MASK_MAX = 80
SEQS = 32
N_DP = 8


def shared_parts(key):
    base_key = jax.random.fold_in(key, 7001)
    dense_matrix = jax.random.truncated_normal(jax.random.fold_in(base_key, 2), -6.0, 6.0, (D, D), jnp.float32) * float(D) ** (-0.5)
    return dense_matrix


def draw_positions(key, part):
    scores = jax.random.randint(key, (SEQS, SEQ_LEN), 0, 1 << 20) * SEQ_LEN + jnp.arange(SEQ_LEN, dtype=jnp.int32)[None, :]
    order = jnp.argsort(scores, axis=1, stable=True)
    return order[:, :MASK_MAX].astype(jnp.int32)


def draw_dense_weight(key, part):
    dense_matrix = shared_parts(key)
    return dense_matrix.astype(jnp.bfloat16)


def draw_hidden(key, part):
    sample_rows = jax.random.truncated_normal(jax.random.fold_in(key, 11), -6.0, 6.0, (SEQS, SEQ_LEN, D), jnp.float32)
    return sample_rows.astype(jnp.bfloat16)


def draw_embedding(key, part):
    table_rows = jax.random.truncated_normal(jax.random.fold_in(key, 21), -6.0, 6.0, (VOCAB, D), jnp.float32) * float(D // 9) ** (-0.5)
    return table_rows.astype(jnp.bfloat16)


def draw_vocab_bias(key, part):
    values_out = jax.random.truncated_normal(jax.random.fold_in(key, 31), -5.0, 5.0, (VOCAB,), jnp.float32)
    return values_out


def place_ends(drawn, stream_key, least, top_value):
    index_at = [jax.random.randint(jax.random.fold_in(stream_key, axis), (), 0, length) for axis, length in enumerate(drawn.shape)]
    widest = drawn.shape.index(max(drawn.shape))
    next_to = index_at[:widest] + [(index_at[widest] + 1) % drawn.shape[widest]] + index_at[widest + 1:]
    return drawn.at[tuple(index_at)].set(least).at[tuple(next_to)].set(top_value)


def rank_table(count, lean):
    portions = [(1 << 20) // math.isqrt(rank ** lean) + 1 for rank in range(1, count + 1)]
    scale = 1 + sum(portions) // (1 << 30)
    return np.cumsum(np.array([max(1, weight // scale) for weight in portions]))


def skewed_ids(rng, extent, number_of, lean):
    grid = rank_table(number_of, lean)
    pick = jax.random.randint(jax.random.fold_in(rng, 1), extent, 0, int(grid[number_of - 1]))
    grade = jnp.searchsorted(jnp.asarray(grid, jnp.int32), pick, side="right")
    return jax.random.permutation(jax.random.fold_in(rng, 2), number_of)[grade].astype(jnp.int32)


def profile(count, total, reach, lean):
    loads = [(1 << 20) // math.isqrt(grade ** lean) + 1 for grade in range(2, count + 1)]
    rest, holding = total - reach - (count - 1), [1] * (count - 1)
    while rest > 0:
        candidates = [i for i in range(count - 1) if holding[i] < reach]
        whole, budget = sum([loads[i] for i in candidates]), rest
        for i in candidates:
            addition = min(reach - holding[i], max(1, budget * loads[i] // whole), rest)
            holding[i] = holding[i] + addition
            rest = rest - addition
    return np.array([reach] + holding)


def ragged(own_key, count, total, bound, slope):
    if count == 2:
        one = jax.random.randint(own_key, (), max(1, total - bound), min(bound, total - 1) + 1)
        return jnp.stack([one, total - one])
    sizes = jnp.asarray(profile(count, total, bound, slope), jnp.int32)
    twos = (count - 1) // 2
    donor, receiver = sizes[1:1 + 2 * twos:2], sizes[2:2 + 2 * twos:2]
    room = jnp.minimum(donor - 1, bound - receiver)
    shifted = jax.random.randint(jax.random.fold_in(own_key, 1), (twos,), 0, 1 << 20) % (room + 1)
    sizes = sizes.at[1:1 + 2 * twos:2].set(donor - shifted).at[2:2 + 2 * twos:2].set(receiver + shifted)
    return sizes[jax.random.permutation(jax.random.fold_in(own_key, 2), count)]


def scatter_about(key, dims, scale, bound, kind=jnp.bfloat16):
    entries = jax.random.normal(key, dims, jnp.float32) * scale
    return jnp.minimum(jnp.maximum(entries, -bound), bound).astype(kind)


def setup_inputs(seed: int = 0) -> dict:
    arg_keys = jax.random.split(jax.random.key(seed), 11)
    return {
        "hidden": draw_hidden(jax.random.fold_in(arg_keys[10], 71), 0),
        "positions": draw_positions(jax.random.fold_in(arg_keys[10], 71), 0),
        "targets": place_ends(skewed_ids(arg_keys[2], (SEQS, MASK_MAX), VOCAB, 2), jax.random.fold_in(arg_keys[2], 3), 0, VOCAB - 1).astype(jnp.int32),
        "counts": ragged(arg_keys[3], SEQS, SEQS * MASK_MAX * 3 // 4, MASK_MAX, 1).astype(jnp.int32),
        "dense_weight": draw_dense_weight(jax.random.fold_in(arg_keys[10], 71), 0),
        "dense_bias": scatter_about(arg_keys[5], (D,), 0.5, 3.0, jnp.float32),
        "norm_gain": jnp.clip(1.0 + 0.12 * jax.random.normal(arg_keys[6], (D,), jnp.float32), 0.4, 1.6),
        "norm_shift": scatter_about(arg_keys[7], (D,), 0.5, 3.0, jnp.float32),
        "embedding": draw_embedding(jax.random.fold_in(arg_keys[10], 71), 0),
        "vocab_bias": draw_vocab_bias(jax.random.fold_in(arg_keys[10], 71), 0),
    }


def transform(rows, dense_weight, dense_bias, norm_gain, norm_shift):
    pre = jnp.dot(rows, dense_weight, preferred_element_type=jnp.float32) + dense_bias
    act = jax.nn.gelu(pre, approximate=False)
    mean = lax.optimization_barrier(jnp.mean(act, axis=-1, keepdims=True))
    centred = act - mean
    var = lax.optimization_barrier(jnp.mean(centred * centred, axis=-1, keepdims=True))
    return (centred * lax.rsqrt(var + 1e-05) * norm_gain + norm_shift).astype(jnp.bfloat16)

def reference(hidden, positions, targets, counts, dense_weight, dense_bias, norm_gain, norm_shift, embedding, vocab_bias):
    width = hidden.shape[2]
    rows = jnp.take_along_axis(hidden, positions[:, :, None], axis=1).reshape(-1, width)
    normed = transform(rows, dense_weight, dense_bias, norm_gain, norm_shift)
    slots = jnp.arange(MASK_MAX, dtype=jnp.int32)
    valid = (slots[None, :] < counts[:, None]).reshape(-1)
    labels = targets.reshape(-1)
    group = normed.shape[0] // N_DP
    vocab_ids = jnp.arange(VOCAB, dtype=jnp.int32)

    def step(carry, block):
        grad_sum, loss_sum = carry
        t_block, label_block, valid_block = block
        logits = lax.dot_general(t_block, embedding, (((1,), (1,)), ((), ())), preferred_element_type=jnp.float32) + vocab_bias
        top = lax.optimization_barrier(jnp.max(logits, axis=1))
        total = lax.optimization_barrier(jnp.sum(jnp.exp(logits - top[:, None]), axis=1))
        lse = top + jnp.log(total)
        onehot = vocab_ids[None, :] == label_block[:, None]
        picked = lax.optimization_barrier(jnp.sum(jnp.where(onehot, logits, 0.0), axis=1))
        loss_sum = loss_sum + jnp.sum(jnp.where(valid_block, lse - picked, 0.0))
        grad_rows = jnp.where(valid_block[:, None], jnp.exp(logits - lse[:, None]) - onehot.astype(jnp.float32), 0.0).astype(jnp.bfloat16)
        grad_sum = grad_sum + lax.dot_general(grad_rows, t_block, (((0,), (0,)), ((), ())), preferred_element_type=jnp.float32)
        return ((grad_sum, loss_sum), None)
    blocks = (normed.reshape(N_DP, group, width), labels.reshape(N_DP, group), valid.reshape(N_DP, group))
    init = (jnp.zeros((VOCAB, width), jnp.float32), jnp.zeros((), jnp.float32))
    (grad_sum, loss_sum), unused = lax.scan(step, init, blocks)
    loss = loss_sum / jnp.sum(counts.astype(jnp.float32))
    return (loss, grad_sum)
```

```python
import math

import jax
import jax.numpy as jnp
from jax import lax
from jax.experimental import pallas as pl
from jax.experimental.pallas import tpu as pltpu
from jax.sharding import PartitionSpec as P


F32, BF16, F16 = jnp.float32, jnp.bfloat16, jnp.float16
ANY = pl.BlockSpec(memory_space=pl.ANY)
WHOLE = pl.BlockSpec(memory_space=pltpu.VMEM)
SCALAR = pl.BlockSpec(memory_space=pltpu.SMEM)


def swap(x, axis, k):
    n = lax.axis_size(axis)
    return lax.ppermute(x, axis, [(a, a ^ k) for a in range(n)])


def transform(rows, dense_weight, dense_bias, norm_gain, norm_shift):
    pre = jnp.dot(rows, dense_weight, preferred_element_type=F32) + dense_bias
    act = jax.nn.gelu(pre, approximate=False)
    mean = jnp.mean(act, axis=-1, keepdims=True)
    centred = act - mean
    var = jnp.mean(centred * centred, axis=-1, keepdims=True)
    return (centred * lax.rsqrt(var + 1e-05) * norm_gain + norm_shift).astype(BF16)


def place(blocks, index, order):
    out = jnp.zeros((len(blocks),) + blocks[0].shape, blocks[0].dtype)
    for block, k in zip(blocks, order):
        out = lax.dynamic_update_index_in_dim(out, block, index ^ k, 0)
    return out


def cost(flops, *arrays):
    moved = sum(math.prod(x.shape) * x.dtype.itemsize for x in arrays)
    return pl.CostEstimate(flops=flops, transcendentals=0, bytes_accessed=moved)


def group_of(chips):
    return 2 if chips % 2 == 0 else 1


def row_copies(group, close, away, rows, core):
    piece = close[0].shape[0]
    copies = []
    for n in range(len(close)):
        for side in range(2):
            start = 2 * piece * (n % group) + (core ^ side) * piece
            spot = pl.ds(pl.multiple_of(start, piece), piece)
            copies.append(((close if side == 0 else away)[n], rows.at[n // group, spot]))
    return copies


def score_rows(where, tables, near, far, bias, labels, begin, before, chips):
    here = len(near)
    piece, width = near[0].shape
    entries, fw = tables[0].shape[-2:]
    split = len(tables)
    group = group_of(here)
    lanes = 2 * piece
    block = lanes * group
    loads = max(1, 2 * (split - 1))
    chunk = math.gcd(block, max(256, (1 << 18) // entries))
    chunk = chunk if chunk % 128 == 0 else block
    chunks = block // chunk
    last = begin + here == chips
    kept = chips if last else here

    def body(where_ref, *refs):
        tabs, refs = refs[:split], refs[split:]
        close, away = refs[:here], refs[here : 2 * here]
        bias_ref, labels_ref, before_ref, out, lse, tail, rows, joined, buffer, sems, out_sems = refs[2 * here :]
        chip, core = where_ref[0], where_ref[1]
        copies = [(tabs[0], joined)] if split == 1 else []
        for n in range(chips if split > 1 else 0):
            for side in range(2):
                spot = pl.ds(pl.multiple_of((2 * (chip ^ n) + (core ^ side)) * fw, fw), fw)
                copies.append((tabs[n].at[core] if side == 0 else tabs[chips].at[n], joined.at[:, spot]))
        copies += row_copies(group, close, away, rows, core)
        copies = [pltpu.make_async_copy(a, b, sems.at[n]) for n, (a, b) in enumerate(copies)]
        for copy in copies:
            copy.start()
        ids = where_ref[2] + lax.broadcasted_iota(jnp.int32, (entries, chunk), 0)
        found = jnp.zeros((1, chunk), F32)
        if last:
            for n in range(begin):
                lse[chip ^ n] = before_ref[n]
        for copy in copies[:loads]:
            copy.wait()
        writes = []
        for g in range(here // group):
            for copy in copies[loads + 2 * group * g : loads + 2 * group * (g + 1)]:
                copy.wait()
            part = []
            label = jnp.concatenate([labels_ref[chip ^ (begin + group * g + n)] for n in range(group)], axis=1)
            for c in range(chunks):
                spot = pl.ds(c * chunk, chunk)
                scores = (
                    lax.dot_general(
                        joined[...], rows[g, spot], (((1,), (1,)), ((), ())), preferred_element_type=F32
                    )
                    + bias_ref[...]
                )
                buffer[g, :, spot] = scores
                write = pltpu.make_async_copy(
                    buffer.at[g, :, spot], out.at[g, :, spot], out_sems.at[g * chunks + c]
                )
                write.start()
                writes.append(write)
                hit = ids == label[:, c * chunk : (c + 1) * chunk]
                found += jnp.sum(jnp.where(hit, scores, 0.0), axis=0, keepdims=True)
                top = jnp.max(scores, axis=0, keepdims=True)
                part.append(top + jnp.log(jnp.sum(jnp.exp(scores - top), axis=0, keepdims=True)))
            part = jnp.concatenate(part, axis=1)
            for n in range(group):
                spot = group * g + n
                lse[chip ^ (begin + spot) if last else spot] = part[:, n * lanes : (n + 1) * lanes]
        tail[...] = jnp.full((1, 128), jnp.sum(found))
        for write in writes:
            write.wait()

    return pl.pallas_call(
        body,
        in_specs=[SCALAR] + [ANY] * (split + 2 * here) + [WHOLE, WHOLE, WHOLE],
        out_specs=[ANY, WHOLE, WHOLE],
        out_shape=[
            jax.ShapeDtypeStruct((here // group, entries, block), F32),
            jax.ShapeDtypeStruct((kept, 1, lanes), F32),
            jax.ShapeDtypeStruct((1, 128), F32),
        ],
        scratch_shapes=[
            pltpu.VMEM((here // group, block, width), BF16),
            pltpu.VMEM((entries, width), BF16),
            pltpu.VMEM((here // group, entries, block), F32),
            pltpu.SemaphoreType.DMA((loads + 2 * here,)),
            pltpu.SemaphoreType.DMA((here // group * chunks,)),
        ],
        cost_estimate=cost(2 * entries * here * lanes * width, *tables, *near, *far),
        name="scores",
    )(where, *tables, *near, *far, bias, labels, before)


def table_grad(where, scores, lse, labels, near, far, fw):
    chips = len(near)
    _, entries, block = scores[0].shape
    piece, width = near[0].shape
    lanes = 2 * piece
    group = block // lanes
    blocks = chips // group
    aligned = fw % 128 == 0
    outs, span = (2 * chips, fw) if aligned else (1, width)
    held = len(scores)

    def body(where_ref, lse_ref, labels_ref, *refs):
        score_refs, refs = refs[:held], refs[held:]
        close, away, refs = refs[:chips], refs[chips : 2 * chips], refs[2 * chips :]
        out, rows, values, total, sems = refs
        chip, core = where_ref[0], where_ref[1]
        sources = [ref.at[g] for ref in score_refs for g in range(ref.shape[0])]
        moves, copies = row_copies(group, close, away, rows, core), []
        for g in range(blocks):
            copies.append((sources[g], values.at[g]))
            copies += moves[2 * group * g : 2 * group * (g + 1)]
        each = 2 * group + 1
        copies = [pltpu.make_async_copy(a, b, sems.at[n]) for n, (a, b) in enumerate(copies)]
        for copy in copies:
            copy.start()
        ids = where_ref[2] + lax.broadcasted_iota(jnp.int32, (entries, block), 0)
        for g in range(blocks):
            chosen = [chip ^ (group * g + n) for n in range(group)]
            label = jnp.concatenate([labels_ref[n] for n in chosen], axis=1)
            norm = jnp.concatenate([lse_ref[n] for n in chosen], axis=1)
            for copy in copies[each * g : each * (g + 1)]:
                copy.wait()
            value = values[g]
            hit = ids == label
            grad = jnp.where(label >= 0, jnp.exp(value - norm) - jnp.where(hit, 1.0, 0.0), 0.0)
            part = jnp.dot(grad.astype(BF16), rows[g], preferred_element_type=F32)
            for s in range(outs):
                spot = slice(s * span, (s + 1) * span)
                if g == 0:
                    total[s] = part[:, spot]
                else:
                    total[s] += part[:, spot]
        peak = jnp.maximum(jnp.max(jnp.abs(total[...])), 1e-30)
        power = jnp.floor(14.0 - jnp.log2(jnp.full((1, 128), 1.0, F32) * peak))
        factor = jnp.exp2(power)[:, :1]
        for s in range(outs):
            out[s, :entries] = total[s] * factor
            out[s, entries:] = jnp.broadcast_to(power[:, :1], (8, span))

    return pl.pallas_call(
        body,
        in_specs=[SCALAR, WHOLE, WHOLE] + [ANY] * (held + 2 * chips),
        out_specs=WHOLE,
        out_shape=jax.ShapeDtypeStruct((outs, entries + 8, span), F32),
        scratch_shapes=[
            pltpu.VMEM((blocks, block, width), BF16),
            pltpu.VMEM((blocks, entries, block), F32),
            pltpu.VMEM((outs, entries, span), F32),
            pltpu.SemaphoreType.DMA((blocks + 2 * chips,)),
        ],
        cost_estimate=cost(2 * entries * chips * lanes * width, *scores, *near, *far),
        name="table_grad",
    )(where, lse, labels, *scores, *near, *far)


def on_device(
    hidden, positions, targets, counts, dense_weight, dense_bias, norm_gain, norm_shift, embedding, vocab_bias
):
    ndp, nmp = lax.axis_size("dp"), lax.axis_size("mp")
    i, j = lax.axis_index("dp").astype(jnp.int32), lax.axis_index("mp").astype(jnp.int32)
    chip, core, chips = i // 2, i % 2, ndp // 2
    everyone = ("dp", "mp")
    own, slots = positions.shape
    width = hidden.shape[2]
    shard, fw = embedding.shape
    entries = shard // ndp
    local = own * slots
    where = jnp.stack([chip, core, j * shard + i * entries])

    slices = embedding.reshape(chips, 2, entries, fw)
    tables = [lax.dynamic_index_in_dim(slices, chip, 0, False)]
    for n in range(1, chips):
        block = lax.dynamic_index_in_dim(slices, chip ^ n, 0, False)
        tables.append(swap(block, "dp", 2 * n))
    stacked = jnp.stack([lax.dynamic_index_in_dim(x, core ^ 1, 0, False) for x in tables])
    far_tables = swap(stacked, "dp", 1)
    aligned = fw % 128 == 0
    if aligned:
        tables = tables + [far_tables]
    else:
        mine = place([lax.dynamic_index_in_dim(x, core, 0, False) for x in tables], chip, list(range(chips)))
        other = place([far_tables[n] for n in range(chips)], chip, list(range(chips)))
        pair = jnp.stack([jnp.where(core == 0, mine, other), jnp.where(core == 0, other, mine)], 1)
        tables = [pair.reshape(ndp, entries, fw).transpose(1, 0, 2).reshape(entries, width)]
    bias = lax.dynamic_slice_in_dim(vocab_bias, i * entries, entries).reshape(entries, 1)

    own_rows = jnp.take_along_axis(hidden, positions[:, :, None], axis=1).reshape(-1, width)
    normed = transform(own_rows, dense_weight, dense_bias, norm_gain, norm_shift)
    zs = list(range(1, nmp))
    column = [normed]
    for k in zs:
        column.append(swap(normed, "mp", k))
    column = place(column, j, [0] + zs).reshape(nmp * local, width)
    near = [column]
    for n in range(1, chips):
        near.append(swap(column, "dp", 2 * n))
    far = [swap(x, "dp", 1) for x in near]
    half = chips // 2 if chips % 4 == 0 else chips
    slot_ids = jnp.arange(slots, dtype=jnp.int32)
    labels = jnp.where(slot_ids[None, :] < counts[:, None], targets, -1).reshape(1, -1)
    labels = jnp.broadcast_to(labels, (ndp * nmp, local))
    labels = lax.all_to_all(labels, everyone, 0, 0, tiled=True)
    labels = labels.reshape(chips, 1, -1)
    scores, lse, found = [], bias, 0.0
    for begin in range(0, chips, half):
        part, lse, tail = score_rows(
            where, tables, near[begin : begin + half], far[begin : begin + half], bias, labels, begin, lse, chips
        )
        scores.append(part)
        found += tail[0, :1]

    count = ndp * nmp * local
    message = jnp.concatenate([lse.reshape(-1), found])
    message = lax.all_to_all(jnp.broadcast_to(message[None], (ndp * nmp,) + message.shape), everyone, 0, 0)
    lse = jax.nn.logsumexp(message[:, :count], axis=0).reshape(chips, 1, -1)
    valid = labels >= 0
    loss = (jnp.sum(jnp.where(valid, lse, 0.0)) - jnp.sum(message[:, count])) / jnp.sum(valid.astype(F32))

    grad = table_grad(where, scores, lse, labels, near, far, fw)
    if not aligned:
        grad = grad.reshape(entries + 8, ndp, fw).transpose(1, 0, 2)
    grad = lax.all_to_all(grad.astype(F16), "dp", 0, 0)
    grad = grad[:, :entries].astype(F32) * jnp.exp2(-grad[:, entries : entries + 1].astype(F32))
    return (loss, grad.reshape(shard, fw))


def solution(mesh):
    in_specs = (
        P(("dp", "mp"), None, None),
        P(("dp", "mp"), None),
        P(("dp", "mp"), None),
        P(("dp", "mp")),
        P(),
        P(),
        P(),
        P(),
        P("mp", "dp"),
        P("mp"),
    )
    out_specs = (P(), P("mp", "dp"))

    return jax.shard_map(on_device, mesh=mesh, in_specs=in_specs, out_specs=out_specs, check_vma=False)
```
